32 devices in a mesh: section: 2 (over core), table: 16 (over z, y, x).
Axes of the slice: x: 2, y: 2, z: 4, core: 2. Of those that a mesh axis runs over, the one named last changes fastest.
Arguments:
- gate_a: bfloat16 [2, 1024, 4096], P('section', 'table'), may hold values from -6 to 6
- cotangent_a: bfloat16 [2, 1024, 4096], P('section', 'table'), may hold values from -6 to 6
- gate_b: bfloat16 [2, 1024, 4096], P('section', 'table'), may hold values from -6 to 6
- table: bfloat16 [1024, 4096], P('table'), may hold values from -6 to 6
- row_ids: int32 [2, 2, 16, 128], P('section', None, 'table'), may hold values from 0 to 1023, as said below
- slots: int32 [2, 2, 1024, 128], P('section', None, 'table'), may hold values from 0 to 127, as said below
- weights: float32 [2, 2, 1024, 128], P('section', None, 'table'), may hold values from 0.02 to 0.2
Outputs:
- mixed_b: bfloat16 [2, 1024, 4096], P('section', 'table')
- grad_gate_a: bfloat16 [2, 1024, 4096], P('section', 'table')
- grad_weights_a: float32 [2, 1024, 128], P('section', 'table')
- grad_table: float32 [1024, 4096], P('table', 'section')
The draws below stay inside these ranges and needn't reach their ends.
Inputs may be any that keep to these rules, and one draw needn't show every extreme that they name: `row_ids`: row r is held by index r // 64 of table. The 128 ids of one list are distinct, and at most 8 of them are held by one index of table; in every section and micro-batch some index of table holds 8 ids of every device's list. `slots`: the 32 picks of one token and head are distinct, and every position of a device's list is picked by some token of that device and micro-batch.
All inputs are finite; a program needn't handle non-finite values.
Results may differ from the reference program's by a relative error of at most 0.0057.
Values may be sent and summed in bfloat16 or wider, within the bound.
A program may use at most 128 MiB of HBM per device.

```python
import math
import jax
import jax.numpy as jnp
from jax import lax

D = 4096
HEADS = 4
TOPK = 32
TOK_DEV = 64
ROWS_DEV = 64
USED = 128
ROW_LIMIT = 8
PICKS = 128
TOKENS = 1024
ROWS = 1024
N_SECTION = 2
N_TABLE = 16


def owner_rows(table_group, device_key):
    popular_key, boost_key = jax.random.split(table_group)
    hottest = jax.random.randint(popular_key, (), 0, N_TABLE)
    score_boost = jax.random.randint(boost_key, (N_TABLE,), 0, 4) * 8192
    scoring_key, key_order, key_shuffle = jax.random.split(device_key, 3)
    row_scores = jax.random.randint(scoring_key, (N_TABLE, ROW_LIMIT), 0, 16384) + score_boost[:, None]
    owner_ids = jnp.arange(N_TABLE, dtype=jnp.int32)
    row_scores = jnp.where(owner_ids[:, None] == hottest, 1 << 17, row_scores)
    ranked = row_scores.reshape(-1) * (N_TABLE * ROW_LIMIT) + jnp.arange(N_TABLE * ROW_LIMIT, dtype=jnp.int32)
    _, chosen = lax.top_k(ranked, USED)
    owner_of = chosen // ROW_LIMIT
    column = chosen % ROW_LIMIT
    order_keys = jax.random.randint(key_order, (N_TABLE, ROWS_DEV), 0, 1 << 16) * ROWS_DEV + jnp.arange(ROWS_DEV, dtype=jnp.int32)[None, :]
    shuffled = jnp.argsort(order_keys, axis=1)
    within = shuffled[owner_of, column]
    listed = owner_of * ROWS_DEV + within
    return listed[jax.random.permutation(key_shuffle, USED)]


def draw_row_ids(key, part):

    def group_lists(index):
        table_group = jax.random.fold_in(key, 7000 + index)

        def one_device(device):
            return owner_rows(table_group, jax.random.fold_in(table_group, 100 + device))
        return jax.vmap(one_device)(jnp.arange(N_TABLE))
    lists = jax.vmap(group_lists)(jnp.arange(N_SECTION * 2))
    return lists.reshape(N_SECTION, 2, N_TABLE, USED).astype(jnp.int32)


def slot_block(block_key):
    key_pairs, key_slots, scoring_key = jax.random.split(block_key, 3)
    pair_rank = jnp.argsort(jax.random.permutation(key_pairs, TOK_DEV * HEADS))
    slot_rank = jnp.argsort(jax.random.permutation(key_slots, USED))
    row_scores = jax.random.randint(scoring_key, (TOK_DEV * HEADS, USED), 0, 1 << 16)
    forced = pair_rank[:, None] == (slot_rank // TOPK)[None, :]
    row_scores = jnp.where(forced, 1 << 17, row_scores)
    ranked = row_scores * USED + jnp.arange(USED, dtype=jnp.int32)[None, :]
    _, picked = lax.top_k(ranked, TOPK)
    return picked.reshape(TOK_DEV, PICKS).astype(jnp.int32)


def draw_slots(key, part):

    def one_block(index):
        return slot_block(jax.random.fold_in(key, 9000 + index))
    blocks = jax.vmap(one_block)(jnp.arange(N_SECTION * 2 * N_TABLE))
    return blocks.reshape(N_SECTION, 2, N_TABLE * TOK_DEV, PICKS)


def level_of(rng, dims, pieces, least, largest):
    level, own = 1.0, jax.random.fold_in(rng, 6)
    for axis_at, shards_of in pieces:
        draws = jnp.exp(jax.random.uniform(jax.random.fold_in(own, axis_at), (shards_of,), jnp.float32, least / len(pieces), largest / len(pieces)))
        level = level * jnp.repeat(draws, dims[axis_at] // shards_of).reshape([-1 if axis == axis_at else 1 for axis in range(len(dims))])
    return level


def scatter_about(rng, extent, scale, most, cuts=(), held_as=jnp.bfloat16):
    gain = level_of(rng, extent, cuts, -0.22, 0.18) if cuts else 1.0
    result = jax.random.normal(rng, extent, jnp.float32) * scale * gain
    return jnp.minimum(jnp.maximum(result, -most), most).astype(held_as)


def setup_inputs(seed: int = 0) -> dict:
    splits = jax.random.split(jax.random.key(seed), 8)
    return {
        "gate_a": scatter_about(splits[0], (N_SECTION, TOKENS, D), 1.0, 6.0, ((0, 2), (1, 16))),
        "cotangent_a": scatter_about(splits[1], (N_SECTION, TOKENS, D), 1.0, 6.0, ((0, 2), (1, 16))),
        "gate_b": scatter_about(splits[2], (N_SECTION, TOKENS, D), 1.0, 6.0, ((0, 2), (1, 16))),
        "table": scatter_about(splits[3], (ROWS, D), 1.0, 6.0, ((0, 16),)),
        "row_ids": draw_row_ids(jax.random.fold_in(splits[7], 71), 0),
        "slots": draw_slots(jax.random.fold_in(splits[7], 71), 0),
        "weights": jnp.clip(jnp.exp(math.log(0.2) - 2.3025851 * jax.random.uniform(splits[6], (N_SECTION, 2, TOKENS, PICKS), jnp.float32) ** level_of(splits[6], (N_SECTION, 2, TOKENS, PICKS), ((0, 2), (2, 16)), -0.2, 0.2)), 0.02, 0.2),
    }


def combine_table(slot_rows, weight_rows, listed):
    matches = slot_rows[:, :, None] == jnp.arange(listed, dtype=jnp.int32)[None, None, :]
    return jnp.sum(jnp.where(matches, weight_rows[:, :, None], jnp.zeros_like(weight_rows[:, :, None])), axis=1).astype(jnp.bfloat16)


def reference(gate_a, cotangent_a, gate_b, table, row_ids, slots, weights):
    section_count = gate_a.shape[0]
    tokens = gate_a.shape[1] // N_TABLE
    features = table.shape[1]

    def split_tokens(values):
        return values.reshape((section_count * N_TABLE, tokens) + values.shape[2:])

    def split_micro(values):
        values = values.reshape(section_count, 2, N_TABLE, tokens, values.shape[-1])
        return jnp.transpose(values, (0, 2, 1, 3, 4)).reshape(section_count * N_TABLE, 2, tokens, values.shape[-1])

    id_lists = jnp.transpose(row_ids, (0, 2, 1, 3)).reshape(section_count * N_TABLE, 2, USED)

    def device_step(grad_table, inputs):
        gate_one, cotangent_one, gate_two, list_pair, slot_pair, weight_pair = inputs
        fetched_a = jnp.take(table, list_pair[0], axis=0)
        fetched_b = jnp.take(table, list_pair[1], axis=0)
        mixing_a = combine_table(slot_pair[0], weight_pair[0], USED)
        mixing_b = combine_table(slot_pair[1], weight_pair[1], USED)
        memory_b = jnp.dot(mixing_b, fetched_b, preferred_element_type=jnp.float32)
        gate_value = gate_two.astype(jnp.float32)
        mixed = (gate_value * jax.nn.sigmoid(gate_value) * memory_b).astype(jnp.bfloat16)
        memory_a = jnp.dot(mixing_a, fetched_a, preferred_element_type=jnp.float32)
        gate_value = gate_one.astype(jnp.float32)
        incoming = cotangent_one.astype(jnp.float32)
        logistic = jax.nn.sigmoid(gate_value)
        grad_gate = (incoming * memory_a * logistic * (1.0 + gate_value * (1.0 - logistic))).astype(jnp.bfloat16)
        grad_memory = (incoming * gate_value * logistic).astype(jnp.bfloat16)
        row_scores = lax.dot_general(grad_memory, fetched_a, (((1,), (1,)), ((), ())), preferred_element_type=jnp.float32)
        grad_weights = jnp.take_along_axis(row_scores, slot_pair[0], axis=1)
        grad_rows = lax.dot_general(mixing_a, grad_memory, (((0,), (0,)), ((), ())), preferred_element_type=jnp.float32).astype(jnp.bfloat16)
        grad_table = grad_table.at[list_pair[0]].add(grad_rows.astype(jnp.float32))
        return grad_table, (mixed, grad_gate, grad_weights)

    inputs = (split_tokens(gate_a), split_tokens(cotangent_a), split_tokens(gate_b), id_lists, split_micro(slots), split_micro(weights))
    grad_table, outputs = lax.scan(device_step, jnp.zeros(table.shape, jnp.float32), inputs)
    mixed, grad_gate, grad_weights = outputs
    mixed = mixed.reshape(section_count, N_TABLE * tokens, features)
    grad_gate = grad_gate.reshape(section_count, N_TABLE * tokens, features)
    grad_weights = grad_weights.reshape(section_count, N_TABLE * tokens, grad_weights.shape[-1])
    return mixed, grad_gate, grad_weights, grad_table
```

```python
import jax
import jax.numpy as jnp
from jax import lax
from jax.sharding import PartitionSpec as P

ROW_LIMIT = 8


def place_rows(row_list, rows_dev, owners, capacity):
    owner_of = row_list // rows_dev
    offset = row_list - owner_of * rows_dev
    listed = row_list.shape[0]
    same = owner_of[:, None] == owner_of[None, :]
    before = jnp.arange(listed)[None, :] < jnp.arange(listed)[:, None]
    position = jnp.sum((same & before).astype(jnp.int32), axis=1)
    place = owner_of * capacity + position
    permute = (place[:, None] == jnp.arange(owners * capacity, dtype=jnp.int32)[None, :])
    requests = jnp.max(jnp.where(permute, offset[:, None], -1), axis=0)
    return requests.reshape(owners, capacity), permute.astype(jnp.bfloat16)


def combine_table(slot_rows, weight_rows, listed):
    matches = slot_rows[:, :, None] == jnp.arange(listed, dtype=jnp.int32)[None, None, :]
    return jnp.sum(
        jnp.where(matches, weight_rows[:, :, None], jnp.zeros_like(weight_rows[:, :, None])), axis=1
    ).astype(jnp.bfloat16)


def local(gate_a, cotangent_a, gate_b, table, row_ids, slots, weights):
    owners = lax.axis_size("table")
    sections = lax.axis_size("section")
    rows_dev, features = table.shape
    listed = row_ids.shape[-1]
    part = features // sections
    requests_a, permute_a = place_rows(row_ids[0, 0, 0], rows_dev, owners, ROW_LIMIT)
    requests_b, permute_b = place_rows(row_ids[0, 1, 0], rows_dev, owners, ROW_LIMIT)
    requests = jnp.stack([requests_a, requests_b], axis=1)
    received = lax.all_to_all(requests, "table", split_axis=0, concat_axis=0, tiled=True)
    asked_a = lax.all_gather(received[:, 0].reshape(-1), "section", axis=0, tiled=True)
    row_index = jnp.arange(rows_dev, dtype=jnp.int32)

    def serve(wanted):
        picks = (wanted.reshape(-1)[:, None] == row_index[None, :]).astype(jnp.bfloat16)
        rows = jnp.dot(picks, table, preferred_element_type=jnp.float32).astype(jnp.bfloat16)
        rows = rows.reshape(owners, ROW_LIMIT, features)
        got = lax.all_to_all(rows, "table", split_axis=0, concat_axis=0, tiled=True)
        return got.reshape(-1, features)

    def placed(mixing, permute):
        return jnp.dot(mixing, permute, preferred_element_type=jnp.float32).astype(jnp.bfloat16)

    mixing_a = placed(combine_table(slots[0, 0], weights[0, 0], listed), permute_a)
    mixing_b = placed(combine_table(slots[0, 1], weights[0, 1], listed), permute_b)
    gate_value = gate_a[0].astype(jnp.float32)
    incoming = cotangent_a[0].astype(jnp.float32)
    logistic = jax.nn.sigmoid(gate_value)
    grad_memory = (incoming * gate_value * logistic).astype(jnp.bfloat16)
    grad_rows = lax.dot_general(
        mixing_a, grad_memory, (((0,), (0,)), ((), ())), preferred_element_type=jnp.float32
    ).astype(jnp.bfloat16)
    outgoing = grad_rows.reshape(owners, ROW_LIMIT, sections, part)
    outgoing = jnp.transpose(outgoing, (2, 0, 1, 3)).reshape(sections * owners, ROW_LIMIT, part)
    arrived = lax.all_to_all(
        outgoing, ("section", "table"), split_axis=0, concat_axis=0, tiled=True
    )
    fetched_a = serve(received[:, 0])
    fetched_b = serve(received[:, 1])
    match = (row_index[:, None] == asked_a[None, :]).astype(jnp.bfloat16)
    grad_table = jnp.dot(match, arrived.reshape(-1, part), preferred_element_type=jnp.float32)
    memory = jnp.dot(mixing_a, fetched_a, preferred_element_type=jnp.float32)
    grad_gate = (incoming * memory * logistic * (1.0 + gate_value * (1.0 - logistic))).astype(
        jnp.bfloat16
    )
    scores = lax.dot_general(
        grad_memory, fetched_a, (((1,), (1,)), ((), ())), preferred_element_type=jnp.float32
    )
    scores = lax.dot_general(
        scores, permute_a.astype(jnp.float32), (((1,), (1,)), ((), ())),
        precision=lax.Precision.HIGHEST, preferred_element_type=jnp.float32,
    )
    chosen = slots[0, 0][:, :, None] == jnp.arange(listed, dtype=jnp.int32)[None, None, :]
    grad_weights = jnp.sum(jnp.where(chosen, scores[:, None, :], 0.0), axis=2)
    memory = jnp.dot(mixing_b, fetched_b, preferred_element_type=jnp.float32)
    gate_value = gate_b[0].astype(jnp.float32)
    mixed_b = (gate_value * jax.nn.sigmoid(gate_value) * memory).astype(jnp.bfloat16)
    return (mixed_b[None], grad_gate[None], grad_weights[None], grad_table)


def solution(mesh):
    return jax.shard_map(
        local,
        mesh=mesh,
        in_specs=(
            P("section", "table", None),
            P("section", "table", None),
            P("section", "table", None),
            P("table", None),
            P("section", None, "table", None),
            P("section", None, "table", None),
            P("section", None, "table", None),
        ),
        out_specs=(
            P("section", "table", None),
            P("section", "table", None),
            P("section", "table", None),
            P("table", "section"),
        ),
        check_vma=False,
    )
```

```python
import jax
import jax.numpy as jnp
from jax import lax
from jax.experimental import pallas as pl
from jax.experimental.pallas import tpu as pltpu
from jax.sharding import PartitionSpec as P

ROW_LIMIT = 8
CHUNK = 512
MESH = pl.DeviceIdType.MESH


def place_rows(row_list, rows_dev, owners, capacity):
    owner_of = row_list // rows_dev
    offset = row_list - owner_of * rows_dev
    listed = row_list.shape[0]
    same = owner_of[:, None] == owner_of[None, :]
    before = jnp.arange(listed)[None, :] < jnp.arange(listed)[:, None]
    position = jnp.sum((same & before).astype(jnp.int32), axis=1)
    place = owner_of * capacity + position
    permute = (place[:, None] == jnp.arange(owners * capacity, dtype=jnp.int32)[None, :])
    requests = jnp.max(jnp.where(permute, offset[:, None], -1), axis=0)
    return requests.reshape(owners, capacity), permute.astype(jnp.bfloat16)


def combine_table(slot_rows, weight_rows, listed):
    matches = slot_rows[:, :, None] == jnp.arange(listed, dtype=jnp.int32)[None, None, :]
    return jnp.sum(
        jnp.where(matches, weight_rows[:, :, None], jnp.zeros_like(weight_rows[:, :, None])), axis=1
    ).astype(jnp.bfloat16)


def drain(block, sem):
    pltpu.make_async_copy(block, block, sem).wait()


def exchange(
    gate_a, cot_a, gate_b, table, asks, mix_a, mix_b, permute, slots,
    mixed_b, grad_gate, grad_weights, grad_table,
    asked, rows_out, fetched, grads_out, arrived, grad_memory, scores,
    ask_send, ask_recv, grad_send, grad_recv, row_send, row_recv,
):
    sections = lax.axis_size("section")
    owners = lax.axis_size("table")
    sec = lax.axis_index("section")
    me = lax.axis_index("table")
    rows_dev, features = table.shape
    part = features // sections
    everyone = sections * owners
    mine = sec * owners + me
    f32 = jnp.float32

    def peers(step, first):
        @pl.loop(first, everyone)
        def _(hop):
            over = lax.rem(mine + hop, everyone)
            step(over // owners, lax.rem(over, owners))

    barrier = pltpu.get_barrier_semaphore()
    peers(
        lambda s, t: pl.semaphore_signal(
            barrier, inc=1, device_id={"section": s, "table": t}, device_id_type=MESH
        ),
        1,
    )

    @pl.loop(0, features // CHUNK)
    def _(c):
        cols = pl.ds(pl.multiple_of(c * CHUNK, CHUNK), CHUNK)
        gate = gate_a[:, cols].astype(f32)
        value = (cot_a[:, cols].astype(f32) * gate * jax.nn.sigmoid(gate)).astype(jnp.bfloat16)
        grad_memory[:, cols] = value
        rows = lax.dot_general(
            mix_a[...], value, (((0,), (0,)), ((), ())), preferred_element_type=f32
        ).reshape(owners, 2, ROW_LIMIT, CHUNK)[:, 0]
        per = part // CHUNK
        inner = pl.ds(pl.multiple_of(lax.rem(c, per) * CHUNK, CHUNK), CHUNK)
        grads_out[c // per, :, :, inner] = rows.astype(jnp.bfloat16)

    pl.semaphore_wait(barrier, everyone - 1)

    def remote(source, target, send, recv, s, t):
        pltpu.make_async_remote_copy(
            src_ref=source, dst_ref=target, send_sem=send, recv_sem=recv,
            device_id={"section": s, "table": t}, device_id_type=MESH,
        ).start()

    peers(lambda s, t: remote(asks.at[t], asked.at[mine], ask_send, ask_recv, s, t), 1)
    pltpu.make_async_copy(asks.at[me], asked.at[mine], ask_recv).start()
    peers(
        lambda s, t: remote(grads_out.at[s, t], arrived.at[mine], grad_send, grad_recv, s, t), 1
    )
    pltpu.make_async_copy(grads_out.at[sec, me], arrived.at[mine], grad_recv).start()

    drain(asked, ask_recv)
    wanted = asked[pl.ds(sec * owners, owners)].reshape(owners * 2 * ROW_LIMIT, -1)[:, :rows_dev]

    @pl.loop(0, features // CHUNK)
    def _(c):
        cols = pl.ds(pl.multiple_of(c * CHUNK, CHUNK), CHUNK)
        rows = jnp.dot(wanted, table[:, cols], preferred_element_type=f32).astype(jnp.bfloat16)
        rows_out[:, :, cols] = rows.reshape(owners, 2 * ROW_LIMIT, CHUNK)

    @pl.loop(1, owners)
    def _(hop):
        t = lax.rem(me + hop, owners)
        remote(rows_out.at[t], fetched.at[me], row_send, row_recv, sec, t)

    pltpu.make_async_copy(rows_out.at[me], fetched.at[me], row_recv).start()

    asked_a = asked[...].astype(f32)[:, :ROW_LIMIT].reshape(everyone * ROW_LIMIT, -1)
    asked_a = asked_a.astype(jnp.bfloat16)
    drain(arrived, grad_recv)

    @pl.loop(0, part // CHUNK)
    def _(c):
        cols = pl.ds(pl.multiple_of(c * CHUNK, CHUNK), CHUNK)
        block = arrived[:, :, cols].reshape(everyone * ROW_LIMIT, CHUNK)
        total = lax.dot_general(
            asked_a, block, (((0,), (0,)), ((), ())), preferred_element_type=f32
        )
        grad_table[:, cols] = total[:rows_dev]

    drain(fetched, row_recv)
    scores[...] = jnp.zeros_like(scores)

    @pl.loop(0, features // CHUNK)
    def _(c):
        cols = pl.ds(pl.multiple_of(c * CHUNK, CHUNK), CHUNK)
        rows = fetched[:, :, cols].reshape(owners * 2 * ROW_LIMIT, CHUNK)
        memory = jnp.dot(mix_a[...], rows, preferred_element_type=f32)
        gate = gate_a[:, cols].astype(f32)
        sig = jax.nn.sigmoid(gate)
        incoming = cot_a[:, cols].astype(f32)
        grad_gate[:, cols] = (incoming * memory * sig * (1.0 + gate * (1.0 - sig))).astype(
            jnp.bfloat16
        )
        scores[...] += lax.dot_general(
            grad_memory[:, cols], rows, (((1,), (1,)), ((), ())), preferred_element_type=f32
        )
        memory = jnp.dot(mix_b[...], rows, preferred_element_type=f32)
        gate = gate_b[:, cols].astype(f32)
        mixed_b[:, cols] = (gate * jax.nn.sigmoid(gate) * memory).astype(jnp.bfloat16)

    listed = lax.dot_general(
        scores[...], permute[...], (((1,), (1,)), ((), ())),
        precision=lax.Precision.HIGHEST, preferred_element_type=f32,
    )
    grad_weights[...] = jnp.take_along_axis(listed, slots[...], axis=1)
    drain(asked.at[pl.ds(0, everyone - 1)], ask_send)
    drain(arrived.at[pl.ds(0, everyone - 1)], grad_send)
    drain(rows_out.at[pl.ds(0, owners - 1)], row_send)


def local(gate_a, cotangent_a, gate_b, table, row_ids, slots, weights):
    owners = lax.axis_size("table")
    sections = lax.axis_size("section")
    rows_dev, features = table.shape
    tokens = gate_a.shape[1]
    listed = row_ids.shape[-1]
    part = features // sections
    lanes = -(-rows_dev // 128) * 128
    requests_a, permute_a = place_rows(row_ids[0, 0, 0], rows_dev, owners, ROW_LIMIT)
    requests_b, permute_b = place_rows(row_ids[0, 1, 0], rows_dev, owners, ROW_LIMIT)
    requests = jnp.concatenate([requests_a, requests_b], axis=1)
    asks = (requests[:, :, None] == jnp.arange(lanes, dtype=jnp.int32)).astype(jnp.bfloat16)

    def widen(permute, which):
        split = permute.reshape(listed, owners, ROW_LIMIT)
        pair = [jnp.zeros_like(split), jnp.zeros_like(split)]
        pair[which] = split
        return jnp.concatenate(pair, axis=2).reshape(listed, owners * 2 * ROW_LIMIT)

    def placed(mixing, permute):
        return jnp.dot(mixing, permute, preferred_element_type=jnp.float32).astype(jnp.bfloat16)

    wide_a, wide_b = widen(permute_a, 0), widen(permute_b, 1)
    mix_a = placed(combine_table(slots[0, 0], weights[0, 0], listed), wide_a)
    mix_b = placed(combine_table(slots[0, 1], weights[0, 1], listed), wide_b)
    bf16 = jnp.bfloat16
    everyone = sections * owners
    vmem = pl.BlockSpec(memory_space=pltpu.VMEM)
    mixed_b, grad_gate, grad_weights, grad_table = pl.pallas_call(
        exchange,
        out_shape=(
            jax.ShapeDtypeStruct((tokens, features), bf16),
            jax.ShapeDtypeStruct((tokens, features), bf16),
            jax.ShapeDtypeStruct((tokens, listed), jnp.float32),
            jax.ShapeDtypeStruct((rows_dev, part), jnp.float32),
        ),
        in_specs=[vmem] * 9,
        out_specs=(vmem,) * 4,
        scratch_shapes=[
            pltpu.VMEM((everyone, 2 * ROW_LIMIT, lanes), bf16),
            pltpu.VMEM((owners, 2 * ROW_LIMIT, features), bf16),
            pltpu.VMEM((owners, 2 * ROW_LIMIT, features), bf16),
            pltpu.VMEM((sections, owners, ROW_LIMIT, part), bf16),
            pltpu.VMEM((everyone, ROW_LIMIT, part), bf16),
            pltpu.VMEM((tokens, features), bf16),
            pltpu.VMEM((tokens, owners * 2 * ROW_LIMIT), jnp.float32),
        ]
        + [pltpu.SemaphoreType.DMA] * 6,
        compiler_params=pltpu.CompilerParams(
            collective_id=0, has_side_effects=True, vmem_limit_bytes=60 * 1024 * 1024
        ),
    )(
        gate_a[0], cotangent_a[0], gate_b[0], table, asks, mix_a, mix_b,
        wide_a.astype(jnp.float32), slots[0, 0],
    )
    return mixed_b[None], grad_gate[None], grad_weights[None], grad_table


def solution(mesh):
    return jax.shard_map(
        local,
        mesh=mesh,
        in_specs=(
            P("section", "table", None),
            P("section", "table", None),
            P("section", "table", None),
            P("table", None),
            P("section", None, "table", None),
            P("section", None, "table", None),
            P("section", None, "table", None),
        ),
        out_specs=(
            P("section", "table", None),
            P("section", "table", None),
            P("section", "table", None),
            P("table", "section"),
        ),
        check_vma=False,
    )
```

```python
import jax
import jax.numpy as jnp
from jax import lax
from jax.experimental import pallas as pl
from jax.experimental.pallas import tpu as pltpu
from jax.sharding import PartitionSpec as P

ROW_LIMIT = 8
CHUNK = 512
GROUP = 8
MESH = pl.DeviceIdType.MESH


def mix_picks(slot_rows, weight_rows):
    picks = slot_rows.shape[1]
    lane = lax.broadcasted_iota(jnp.int32, slot_rows.shape, 1)

    def group(_, carry):
        slot, weight, total = carry
        for p in range(GROUP):
            hit = slot[:, p : p + 1] == lane
            total = total + jnp.where(hit, weight[:, p : p + 1], 0.0)
        return (
            pltpu.roll(slot, picks - GROUP, 1), pltpu.roll(weight, picks - GROUP, 1), total
        )

    start = (slot_rows, weight_rows, jnp.zeros(weight_rows.shape, jnp.float32))
    return lax.fori_loop(0, picks // GROUP, group, start)[2].astype(jnp.bfloat16)


def place_rows(ids, owners, rows_dev, lanes, base):
    listed = ids.shape[1]
    f32, bf16 = jnp.float32, jnp.bfloat16
    owner = lax.broadcasted_iota(jnp.int32, (owners, listed), 0)
    first = owner * rows_dev
    member = ((ids >= first) & (ids < first + rows_dev)).astype(f32)
    before = lax.broadcasted_iota(jnp.int32, (listed, listed), 0) < lax.broadcasted_iota(
        jnp.int32, (listed, listed), 1
    )
    earlier = jnp.dot(
        member.astype(bf16), before.astype(f32).astype(bf16), preferred_element_type=f32
    )
    spot = earlier + (owner * (2 * ROW_LIMIT) + base).astype(f32)
    place = jnp.sum(member * spot, axis=0, keepdims=True).astype(jnp.int32)
    offset = ids - jnp.sum(member * first.astype(f32), axis=0, keepdims=True).astype(jnp.int32)
    space = lax.broadcasted_iota(jnp.int32, (owners * 2 * ROW_LIMIT, listed), 0)
    wide = (space == place).astype(f32).astype(bf16)
    row = lax.broadcasted_iota(jnp.int32, (lanes, listed), 0)
    held = (row == offset).astype(f32).astype(bf16)
    ask = lax.dot_general(wide, held, (((1,), (1,)), ((), ())), preferred_element_type=f32)
    return wide, ask


def spread(mixing, wide):
    return lax.dot_general(
        mixing, wide, (((1,), (1,)), ((), ())), preferred_element_type=jnp.float32
    ).astype(jnp.bfloat16)


def drain(block, sem):
    pltpu.make_async_copy(block, block, sem).wait()


def exchange(
    gate_a, cot_a, gate_b, table, row_ids, slots, weights,
    mixed_b, grad_gate, grad_weights, grad_table,
    asks, mix_a, asked, rows_out, fetched, grads_out, arrived, grad_memory, scores,
    ask_send, ask_recv, grad_send, grad_recv, row_send, row_recv,
):
    sections = lax.axis_size("section")
    owners = lax.axis_size("table")
    sec = lax.axis_index("section")
    me = lax.axis_index("table")
    rows_dev, features = table.shape
    part = features // sections
    everyone = sections * owners
    mine = sec * owners + me
    f32 = jnp.float32

    def peers(step, first):
        @pl.loop(first, everyone)
        def _(hop):
            over = lax.rem(mine + hop, everyone)
            step(over // owners, lax.rem(over, owners))

    barrier = pltpu.get_barrier_semaphore()
    peers(
        lambda s, t: pl.semaphore_signal(
            barrier, inc=1, device_id={"section": s, "table": t}, device_id_type=MESH
        ),
        1,
    )

    lanes = asks.shape[-1]
    ids = row_ids[...]
    wide_a, ask_a = place_rows(ids[0:1], owners, rows_dev, lanes, 0)
    wide_b, ask_b = place_rows(ids[1:2], owners, rows_dev, lanes, ROW_LIMIT)
    asks[...] = (ask_a + ask_b).astype(jnp.bfloat16).reshape(asks.shape)
    pl.semaphore_wait(barrier, everyone - 1)

    def remote(source, target, send, recv, s, t):
        pltpu.make_async_remote_copy(
            src_ref=source, dst_ref=target, send_sem=send, recv_sem=recv,
            device_id={"section": s, "table": t}, device_id_type=MESH,
        ).start()

    peers(lambda s, t: remote(asks.at[t], asked.at[mine], ask_send, ask_recv, s, t), 1)
    pltpu.make_async_copy(asks.at[me], asked.at[mine], ask_recv).start()
    mix_a[...] = spread(mix_picks(slots[0], weights[0]), wide_a)

    @pl.loop(0, features // CHUNK)
    def _(c):
        cols = pl.ds(pl.multiple_of(c * CHUNK, CHUNK), CHUNK)
        gate = gate_a[:, cols].astype(f32)
        value = (cot_a[:, cols].astype(f32) * gate * jax.nn.sigmoid(gate)).astype(jnp.bfloat16)
        grad_memory[:, cols] = value
        rows = lax.dot_general(
            mix_a[...], value, (((0,), (0,)), ((), ())), preferred_element_type=f32
        ).reshape(owners, 2, ROW_LIMIT, CHUNK)[:, 0]
        per = part // CHUNK
        inner = pl.ds(pl.multiple_of(lax.rem(c, per) * CHUNK, CHUNK), CHUNK)
        grads_out[c // per, :, :, inner] = rows.astype(jnp.bfloat16)

    peers(
        lambda s, t: remote(grads_out.at[s, t], arrived.at[mine], grad_send, grad_recv, s, t), 1
    )
    pltpu.make_async_copy(grads_out.at[sec, me], arrived.at[mine], grad_recv).start()

    drain(asked, ask_recv)
    wanted = asked[pl.ds(sec * owners, owners)].reshape(owners * 2 * ROW_LIMIT, -1)[:, :rows_dev]

    @pl.loop(0, features // CHUNK)
    def _(c):
        cols = pl.ds(pl.multiple_of(c * CHUNK, CHUNK), CHUNK)
        rows = jnp.dot(wanted, table[:, cols], preferred_element_type=f32).astype(jnp.bfloat16)
        rows_out[:, :, cols] = rows.reshape(owners, 2 * ROW_LIMIT, CHUNK)

    @pl.loop(1, owners)
    def _(hop):
        t = lax.rem(me + hop, owners)
        remote(rows_out.at[t], fetched.at[me], row_send, row_recv, sec, t)

    pltpu.make_async_copy(rows_out.at[me], fetched.at[me], row_recv).start()

    mix_b = spread(mix_picks(slots[1], weights[1]), wide_b)
    asked_a = asked[...].astype(f32)[:, :ROW_LIMIT].reshape(everyone * ROW_LIMIT, -1)
    asked_a = asked_a.astype(jnp.bfloat16)
    drain(arrived, grad_recv)

    @pl.loop(0, part // CHUNK)
    def _(c):
        cols = pl.ds(pl.multiple_of(c * CHUNK, CHUNK), CHUNK)
        block = arrived[:, :, cols].reshape(everyone * ROW_LIMIT, CHUNK)
        total = lax.dot_general(
            asked_a, block, (((0,), (0,)), ((), ())), preferred_element_type=f32
        )
        grad_table[:, cols] = total[:rows_dev]

    drain(fetched, row_recv)
    scores[...] = jnp.zeros_like(scores)

    @pl.loop(0, features // CHUNK)
    def _(c):
        cols = pl.ds(pl.multiple_of(c * CHUNK, CHUNK), CHUNK)
        rows = fetched[:, :, cols].reshape(owners * 2 * ROW_LIMIT, CHUNK)
        memory = jnp.dot(mix_a[...], rows, preferred_element_type=f32)
        gate = gate_a[:, cols].astype(f32)
        sig = jax.nn.sigmoid(gate)
        incoming = cot_a[:, cols].astype(f32)
        grad_gate[:, cols] = (incoming * memory * sig * (1.0 + gate * (1.0 - sig))).astype(
            jnp.bfloat16
        )
        scores[...] += lax.dot_general(
            grad_memory[:, cols], rows, (((1,), (1,)), ((), ())), preferred_element_type=f32
        )
        memory = jnp.dot(mix_b, rows, preferred_element_type=f32)
        gate = gate_b[:, cols].astype(f32)
        mixed_b[:, cols] = (gate * jax.nn.sigmoid(gate) * memory).astype(jnp.bfloat16)

    listed = lax.dot_general(
        scores[...], wide_a.astype(f32), (((1,), (0,)), ((), ())),
        precision=lax.Precision.HIGHEST, preferred_element_type=f32,
    )
    grad_weights[...] = jnp.take_along_axis(listed, slots[0], axis=1)
    drain(asked.at[pl.ds(0, everyone - 1)], ask_send)
    drain(arrived.at[pl.ds(0, everyone - 1)], grad_send)
    drain(rows_out.at[pl.ds(0, owners - 1)], row_send)


def local(gate_a, cotangent_a, gate_b, table, row_ids, slots, weights):
    owners = lax.axis_size("table")
    sections = lax.axis_size("section")
    rows_dev, features = table.shape
    tokens = gate_a.shape[1]
    listed = row_ids.shape[-1]
    part = features // sections
    lanes = -(-rows_dev // 128) * 128
    bf16 = jnp.bfloat16
    everyone = sections * owners
    vmem = pl.BlockSpec(memory_space=pltpu.VMEM)
    mixed_b, grad_gate, grad_weights, grad_table = pl.pallas_call(
        exchange,
        out_shape=(
            jax.ShapeDtypeStruct((tokens, features), bf16),
            jax.ShapeDtypeStruct((tokens, features), bf16),
            jax.ShapeDtypeStruct((tokens, listed), jnp.float32),
            jax.ShapeDtypeStruct((rows_dev, part), jnp.float32),
        ),
        in_specs=[vmem] * 7,
        out_specs=(vmem,) * 4,
        scratch_shapes=[
            pltpu.VMEM((owners, 2 * ROW_LIMIT, lanes), bf16),
            pltpu.VMEM((tokens, owners * 2 * ROW_LIMIT), bf16),
            pltpu.VMEM((everyone, 2 * ROW_LIMIT, lanes), bf16),
            pltpu.VMEM((owners, 2 * ROW_LIMIT, features), bf16),
            pltpu.VMEM((owners, 2 * ROW_LIMIT, features), bf16),
            pltpu.VMEM((sections, owners, ROW_LIMIT, part), bf16),
            pltpu.VMEM((everyone, ROW_LIMIT, part), bf16),
            pltpu.VMEM((tokens, features), bf16),
            pltpu.VMEM((tokens, owners * 2 * ROW_LIMIT), jnp.float32),
        ]
        + [pltpu.SemaphoreType.DMA] * 6,
        compiler_params=pltpu.CompilerParams(
            collective_id=0, has_side_effects=True, vmem_limit_bytes=60 * 1024 * 1024
        ),
    )(
        gate_a[0], cotangent_a[0], gate_b[0], table, row_ids[0, :, 0], slots[0], weights[0]
    )
    return mixed_b[None], grad_gate[None], grad_weights[None], grad_table


def solution(mesh):
    return jax.shard_map(
        local,
        mesh=mesh,
        in_specs=(
            P("section", "table", None),
            P("section", "table", None),
            P("section", "table", None),
            P("table", None),
            P("section", None, "table", None),
            P("section", None, "table", None),
            P("section", None, "table", None),
        ),
        out_specs=(
            P("section", "table", None),
            P("section", "table", None),
            P("section", "table", None),
            P("table", "section"),
        ),
        check_vma=False,
    )
```

```python
import jax
import jax.numpy as jnp
from jax import lax
from jax.experimental import pallas as pl
from jax.experimental.pallas import tpu as pltpu
from jax.sharding import PartitionSpec as P

ROW_LIMIT = 8
CHUNK = 512
GROUP = 8
MESH = pl.DeviceIdType.MESH


def mix_picks(slot_rows, weight_rows):
    picks = slot_rows.shape[1]
    lane = lax.broadcasted_iota(jnp.int32, slot_rows.shape, 1)

    def group(_, carry):
        slot, weight, total = carry
        for p in range(GROUP):
            hit = slot[:, p : p + 1] == lane
            total = total + jnp.where(hit, weight[:, p : p + 1], 0.0)
        return (
            pltpu.roll(slot, picks - GROUP, 1), pltpu.roll(weight, picks - GROUP, 1), total
        )

    start = (slot_rows, weight_rows, jnp.zeros(weight_rows.shape, jnp.float32))
    return lax.fori_loop(0, picks // GROUP, group, start)[2].astype(jnp.bfloat16)


def place_rows(ids, owners, rows_dev, lanes, base):
    listed = ids.shape[1]
    f32, bf16 = jnp.float32, jnp.bfloat16
    owner = lax.broadcasted_iota(jnp.int32, (owners, listed), 0)
    first = owner * rows_dev
    member = ((ids >= first) & (ids < first + rows_dev)).astype(f32)
    before = lax.broadcasted_iota(jnp.int32, (listed, listed), 0) < lax.broadcasted_iota(
        jnp.int32, (listed, listed), 1
    )
    earlier = jnp.dot(
        member.astype(bf16), before.astype(f32).astype(bf16), preferred_element_type=f32
    )
    spot = earlier + (owner * (2 * ROW_LIMIT) + base).astype(f32)
    place = jnp.sum(member * spot, axis=0, keepdims=True).astype(jnp.int32)
    offset = ids - jnp.sum(member * first.astype(f32), axis=0, keepdims=True).astype(jnp.int32)
    space = lax.broadcasted_iota(jnp.int32, (owners * 2 * ROW_LIMIT, listed), 0)
    wide = (space == place).astype(f32).astype(bf16)
    row = lax.broadcasted_iota(jnp.int32, (lanes, listed), 0)
    held = (row == offset).astype(f32).astype(bf16)
    ask = lax.dot_general(wide, held, (((1,), (1,)), ((), ())), preferred_element_type=f32)
    return wide, ask


def spread(mixing, wide):
    return lax.dot_general(
        mixing, wide, (((1,), (1,)), ((), ())), preferred_element_type=jnp.float32
    ).astype(jnp.bfloat16)


def drain(block, sem):
    pltpu.make_async_copy(block, block, sem).wait()


def exchange(
    gate_a, cot_a, gate_b, table, row_ids, slots, weights,
    mixed_b, grad_gate, grad_weights, grad_table,
    asks, mix_a, asked, rows_out, fetched, grads_out, arrived, grad_memory, scores,
    table_far, asked_far,
    ask_send, ask_recv, grad_send, grad_recv, row_send, row_recv,
    table_send, table_recv, far_send, far_recv,
):
    sections = lax.axis_size("section")
    owners = lax.axis_size("table")
    sec = lax.axis_index("section")
    me = lax.axis_index("table")
    rows_dev, features = table.shape
    part = features // sections
    everyone = sections * owners
    mine = sec * owners + me
    half = owners // 2
    seat = lax.rem(me, half)
    low = me - seat
    twin = lax.rem(me + half, owners)
    f32 = jnp.float32

    def peers(step, first):
        @pl.loop(first, everyone)
        def _(hop):
            over = lax.rem(mine + hop, everyone)
            step(over // owners, lax.rem(over, owners))

    barrier = pltpu.get_barrier_semaphore()
    peers(
        lambda s, t: pl.semaphore_signal(
            barrier, inc=1, device_id={"section": s, "table": t}, device_id_type=MESH
        ),
        1,
    )

    lanes = asks.shape[-1]
    ids = row_ids[...]
    wide_a, ask_a = place_rows(ids[0:1], owners, rows_dev, lanes, 0)
    wide_b, ask_b = place_rows(ids[1:2], owners, rows_dev, lanes, ROW_LIMIT)
    asks[...] = (ask_a + ask_b).astype(jnp.bfloat16).reshape(asks.shape)
    pl.semaphore_wait(barrier, everyone - 1)

    def remote(source, target, send, recv, s, t):
        pltpu.make_async_remote_copy(
            src_ref=source, dst_ref=target, send_sem=send, recv_sem=recv,
            device_id={"section": s, "table": t}, device_id_type=MESH,
        ).start()

    peers(lambda s, t: remote(asks.at[t], asked.at[mine], ask_send, ask_recv, s, t), 1)
    pltpu.make_async_copy(asks.at[me], asked.at[mine], ask_recv).start()

    @pl.loop(1, half)
    def _(hop):
        t = low + lax.rem(seat + hop, half)
        other = lax.rem(t + half, owners)
        remote(asks.at[other], asked_far.at[seat], far_send, far_recv, sec, t)

    pltpu.make_async_copy(asks.at[twin], asked_far.at[seat], far_recv).start()
    remote(table, table_far, table_send, table_recv, sec, twin)
    mix_a[...] = spread(mix_picks(slots[0], weights[0]), wide_a)

    @pl.loop(0, features // CHUNK)
    def _(c):
        cols = pl.ds(pl.multiple_of(c * CHUNK, CHUNK), CHUNK)
        gate = gate_a[:, cols].astype(f32)
        value = (cot_a[:, cols].astype(f32) * gate * jax.nn.sigmoid(gate)).astype(jnp.bfloat16)
        grad_memory[:, cols] = value
        rows = lax.dot_general(
            mix_a[...], value, (((0,), (0,)), ((), ())), preferred_element_type=f32
        ).reshape(owners, 2, ROW_LIMIT, CHUNK)[:, 0]
        per = part // CHUNK
        inner = pl.ds(pl.multiple_of(lax.rem(c, per) * CHUNK, CHUNK), CHUNK)
        grads_out[c // per, :, :, inner] = rows.astype(jnp.bfloat16)

    peers(
        lambda s, t: remote(grads_out.at[s, t], arrived.at[mine], grad_send, grad_recv, s, t), 1
    )
    pltpu.make_async_copy(grads_out.at[sec, me], arrived.at[mine], grad_recv).start()

    drain(asked, ask_recv)
    drain(asked_far, far_recv)

    def serve(wanted, rows_ref, side, place):
        wanted = wanted.reshape(half * 2 * ROW_LIMIT, -1)[:, :rows_dev]

        @pl.loop(0, features // CHUNK)
        def _(c):
            cols = pl.ds(pl.multiple_of(c * CHUNK, CHUNK), CHUNK)
            rows = jnp.dot(wanted, rows_ref[:, cols], preferred_element_type=f32)
            rows = rows.astype(jnp.bfloat16).reshape(half, 2 * ROW_LIMIT, CHUNK)
            rows_out[side, :, :, cols] = rows

        @pl.loop(1, half)
        def _(hop):
            spot = lax.rem(seat + hop, half)
            remote(
                rows_out.at[side, spot], fetched.at[place], row_send, row_recv, sec, low + spot
            )

        pltpu.make_async_copy(rows_out.at[side, seat], fetched.at[place], row_recv).start()

    serve(asked[pl.ds(sec * owners + low, half)], table, 0, me)
    drain(table_far, table_recv)
    serve(asked_far[...], table_far, 1, twin)

    mix_b = spread(mix_picks(slots[1], weights[1]), wide_b)
    asked_a = asked[...].astype(f32)[:, :ROW_LIMIT].reshape(everyone * ROW_LIMIT, -1)
    asked_a = asked_a.astype(jnp.bfloat16)
    drain(arrived, grad_recv)

    @pl.loop(0, part // CHUNK)
    def _(c):
        cols = pl.ds(pl.multiple_of(c * CHUNK, CHUNK), CHUNK)
        block = arrived[:, :, cols].reshape(everyone * ROW_LIMIT, CHUNK)
        total = lax.dot_general(
            asked_a, block, (((0,), (0,)), ((), ())), preferred_element_type=f32
        )
        grad_table[:, cols] = total[:rows_dev]

    drain(fetched, row_recv)
    scores[...] = jnp.zeros_like(scores)

    @pl.loop(0, features // CHUNK)
    def _(c):
        cols = pl.ds(pl.multiple_of(c * CHUNK, CHUNK), CHUNK)
        rows = fetched[:, :, cols].reshape(owners * 2 * ROW_LIMIT, CHUNK)
        memory = jnp.dot(mix_a[...], rows, preferred_element_type=f32)
        gate = gate_a[:, cols].astype(f32)
        sig = jax.nn.sigmoid(gate)
        incoming = cot_a[:, cols].astype(f32)
        grad_gate[:, cols] = (incoming * memory * sig * (1.0 + gate * (1.0 - sig))).astype(
            jnp.bfloat16
        )
        scores[...] += lax.dot_general(
            grad_memory[:, cols], rows, (((1,), (1,)), ((), ())), preferred_element_type=f32
        )
        memory = jnp.dot(mix_b, rows, preferred_element_type=f32)
        gate = gate_b[:, cols].astype(f32)
        mixed_b[:, cols] = (gate * jax.nn.sigmoid(gate) * memory).astype(jnp.bfloat16)

    listed = lax.dot_general(
        scores[...], wide_a.astype(f32), (((1,), (0,)), ((), ())),
        precision=lax.Precision.HIGHEST, preferred_element_type=f32,
    )
    grad_weights[...] = jnp.take_along_axis(listed, slots[0], axis=1)
    drain(asked.at[pl.ds(0, everyone - 1)], ask_send)
    drain(arrived.at[pl.ds(0, everyone - 1)], grad_send)
    drain(rows_out.at[:, pl.ds(0, half - 1)], row_send)
    drain(asked_far.at[pl.ds(0, half - 1)], far_send)
    drain(table_far, table_send)


def local(gate_a, cotangent_a, gate_b, table, row_ids, slots, weights):
    owners = lax.axis_size("table")
    sections = lax.axis_size("section")
    rows_dev, features = table.shape
    tokens = gate_a.shape[1]
    listed = row_ids.shape[-1]
    part = features // sections
    lanes = -(-rows_dev // 128) * 128
    bf16 = jnp.bfloat16
    everyone = sections * owners
    vmem = pl.BlockSpec(memory_space=pltpu.VMEM)
    mixed_b, grad_gate, grad_weights, grad_table = pl.pallas_call(
        exchange,
        out_shape=(
            jax.ShapeDtypeStruct((tokens, features), bf16),
            jax.ShapeDtypeStruct((tokens, features), bf16),
            jax.ShapeDtypeStruct((tokens, listed), jnp.float32),
            jax.ShapeDtypeStruct((rows_dev, part), jnp.float32),
        ),
        in_specs=[vmem] * 7,
        out_specs=(vmem,) * 4,
        scratch_shapes=[
            pltpu.VMEM((owners, 2 * ROW_LIMIT, lanes), bf16),
            pltpu.VMEM((tokens, owners * 2 * ROW_LIMIT), bf16),
            pltpu.VMEM((everyone, 2 * ROW_LIMIT, lanes), bf16),
            pltpu.VMEM((2, owners // 2, 2 * ROW_LIMIT, features), bf16),
            pltpu.VMEM((owners, 2 * ROW_LIMIT, features), bf16),
            pltpu.VMEM((sections, owners, ROW_LIMIT, part), bf16),
            pltpu.VMEM((everyone, ROW_LIMIT, part), bf16),
            pltpu.VMEM((tokens, features), bf16),
            pltpu.VMEM((tokens, owners * 2 * ROW_LIMIT), jnp.float32),
            pltpu.VMEM((rows_dev, features), bf16),
            pltpu.VMEM((owners // 2, 2 * ROW_LIMIT, lanes), bf16),
        ]
        + [pltpu.SemaphoreType.DMA] * 10,
        compiler_params=pltpu.CompilerParams(
            collective_id=0, has_side_effects=True, vmem_limit_bytes=60 * 1024 * 1024
        ),
    )(
        gate_a[0], cotangent_a[0], gate_b[0], table, row_ids[0, :, 0], slots[0], weights[0]
    )
    return mixed_b[None], grad_gate[None], grad_weights[None], grad_table


def solution(mesh):
    return jax.shard_map(
        local,
        mesh=mesh,
        in_specs=(
            P("section", "table", None),
            P("section", "table", None),
            P("section", "table", None),
            P("table", None),
            P("section", None, "table", None),
            P("section", None, "table", None),
            P("section", None, "table", None),
        ),
        out_specs=(
            P("section", "table", None),
            P("section", "table", None),
            P("section", "table", None),
            P("table", "section"),
        ),
        check_vma=False,
    )
```
